128 devices in a mesh: row: 8 (over z, core), col: 16 (over y, x).
Axes of the slice: x: 4, y: 4, z: 4, core: 2. Of those that a mesh axis runs over, the one named last changes fastest.
Arguments:
- singles: bfloat16 [1024, 384], P('row', 'col'), may hold values from -6 to 6
- pair_in: bfloat16 [1024, 1024, 128], P('row', 'col'), may hold values from -6 to 6
- proj_weight: bfloat16 [384, 256], P('col'), may hold values from -0.3125 to 0.3125
- gain_first: float32 [128], replicated, may hold values from 0.1 to 1.9
- first_in: bfloat16 [128, 1024], replicated, may hold values from -0.5 to 0.5
- first_out: bfloat16 [512, 128], replicated, may hold values from -0.25 to 0.25
- gain_second: float32 [128], replicated, may hold values from 0.1 to 1.9
- second_in: bfloat16 [128, 1024], replicated, may hold values from -0.5 to 0.5
- second_out: bfloat16 [512, 128], replicated, may hold values from -0.25 to 0.25
- head_weight: bfloat16 [128, 64], replicated, may hold values from -1.5 to 1.5
- pae_bins: int32 [1024, 1024], P('row', 'col'), may hold values from 0 to 63
- chain_perm: int32 [1024], replicated, may hold values from 0 to 1023, as said below
- resolved_counts: int32 [8, 16], P('row'), may hold values from 1 to 256, 2048 in all within a row
- tile_order: int32 [8, 4096], P('row', 'col'), may hold values from 0 to 255, as said below
Outputs:
- pair_grad: bfloat16 [1024, 1024, 128], P('row', 'col')
- single_grad: float32 [1024, 384], P('row', 'col')
- second_in_grad: float32 [128, 1024], replicated
- second_out_grad: float32 [512, 128], replicated
- head_grad: float32 [128, 64], replicated
The draws below stay inside these ranges and needn't reach their ends.
Inputs may be any that keep to these rules, and one draw needn't show every extreme that they name: chain_perm maps every aligned group of 64 tokens onto itself, moving whole aligned runs of 16 tokens and keeping the order inside a run. Each row of resolved_counts sums to 2048, and its largest entry is 256. In each row of tile_order, entries b * 256 to (b + 1) * 256 - 1 are a permutation of 0 to 255.
All inputs are finite; a program needn't handle non-finite values.
Results may differ from the reference program's by a relative error of at most 0.011.
Values may be sent and summed in bfloat16 or wider, within the bound.
A program may use at most 64 MiB of HBM per device.

```python
import math
import jax
import jax.numpy as jnp
import numpy as np
from jax import lax

CS = 384
CZ = 128
HID = 512
BINS = 64
TILE = 32
CHAIN = 16
GROUP = 64
R_DEV = 128
C_DEV = 64
N = 1024
TILES_DEV = 256
RES_DEV = 128
N_ROW = 8
N_COL = 16


def draw_chain_perm(key, part):
    group_count = N // GROUP
    chain_count = GROUP // CHAIN
    scores = jax.random.randint(key, (group_count, chain_count), 0, 1 << 20) * chain_count + jnp.arange(chain_count, dtype=jnp.int32)[None, :]
    shuffled = jnp.argsort(scores, axis=1).astype(jnp.int32)
    tokens = jnp.arange(group_count, dtype=jnp.int32)[:, None, None] * GROUP + shuffled[:, :, None] * CHAIN + jnp.arange(CHAIN, dtype=jnp.int32)[None, None, :]
    return tokens.reshape(N).astype(jnp.int32)


def draw_tile_order(key, part):
    device_count = N_ROW * N_COL
    scores = jax.random.randint(key, (device_count, TILES_DEV), 0, 1 << 20) * TILES_DEV + jnp.arange(TILES_DEV, dtype=jnp.int32)[None, :]
    ordered = jnp.argsort(scores, axis=1).astype(jnp.int32)
    return ordered.reshape(N_ROW, N_COL * TILES_DEV)


def touch_ends(values, own_key, low, top_value):
    longest = values.shape.index(max(values.shape))
    spots = []
    for shift in (0, 1):
        where = [jax.random.randint(jax.random.fold_in(own_key, axis), (), 0, length) for axis, length in enumerate(values.shape)]
        where[longest] = (where[longest] + shift) % values.shape[longest]
        spots.append(tuple(where))
    return values.at[spots[0]].set(low).at[spots[1]].set(top_value)


def steps_of(rng, dims, split, low, high):
    def one(axis_at, parts):
        heights = jax.random.uniform(jax.random.fold_in(jax.random.fold_in(rng, 6), axis_at), (parts,), jnp.float32, low / len(split), high / len(split))
        return jnp.repeat(jnp.exp(heights), dims[axis_at] // parts).reshape((-1,) + (1,) * (len(dims) - axis_at - 1))

    level = one(*split[0])
    for cut in split[1:]:
        level = level * one(*cut)
    return level


def length_profile(count, total, most, lean):
    weights = [(1 << 20) // math.isqrt(rank ** lean) + 1 for rank in range(2, count + 1)]
    surplus, holding = total - most - (count - 1), [1] * (count - 1)
    while surplus > 0:
        free = [i for i in range(count - 1) if holding[i] < most]
        pool, remaining = sum([weights[i] for i in free]), surplus
        for i in free:
            more = min(most - holding[i], max(1, remaining * weights[i] // pool), surplus)
            holding[i] = holding[i] + more
            surplus = surplus - more
    return np.array([most] + holding)


def uneven_parts(stream_key, number_of, total, bound, slope):
    if number_of == 2:
        one = jax.random.randint(stream_key, (), max(1, total - bound), min(bound, total - 1) + 1)
        return jnp.stack([one, total - one])
    sizes = jnp.asarray(length_profile(number_of, total, bound, slope), jnp.int32)
    pairs = (number_of - 1) // 2
    giver, taker = sizes[1:1 + 2 * pairs:2], sizes[2:2 + 2 * pairs:2]
    room = jnp.minimum(giver - 1, bound - taker)
    shifted = jax.random.randint(jax.random.fold_in(stream_key, 1), (pairs,), 0, 1 << 20) % (room + 1)
    sizes = sizes.at[1:1 + 2 * pairs:2].set(giver - shifted).at[2:2 + 2 * pairs:2].set(taker + shifted)
    return sizes[jax.random.permutation(jax.random.fold_in(stream_key, 2), number_of)]


def bell_draw(rng, shape, scale, limit, split=(), kind=jnp.bfloat16):
    loudness = steps_of(rng, shape, split, -0.22, 0.18) if split else 1.0
    array = jax.random.normal(rng, shape, jnp.float32) * scale * loudness
    return jnp.minimum(jnp.maximum(array, -limit), limit).astype(kind)


def setup_inputs(seed: int = 0) -> dict:
    keys = jax.random.split(jax.random.key(seed), 15)
    singles = bell_draw(keys[0], (N, CS), 1.0, 6.0, ((0, 8), (1, 16)))
    pair_in = bell_draw(keys[1], (N, N, CZ), 1.0, 6.0, ((0, 8), (1, 16)))
    proj_weight = bell_draw(keys[2], (CS, 2 * CZ), CS ** -0.5, 0.3125, ((0, 16),))
    gain_first = jnp.clip(1.0 + 0.18 * jax.random.normal(keys[3], (CZ,), jnp.float32), 0.1, 1.9)
    first_in = bell_draw(keys[4], (CZ, 2 * HID), CZ ** -0.5, 0.5)
    first_out = bell_draw(keys[5], (HID, CZ), HID ** -0.5, 0.25)
    gain_second = jnp.clip(1.0 + 0.18 * jax.random.normal(keys[6], (CZ,), jnp.float32), 0.1, 1.9)
    second_in = bell_draw(keys[7], (CZ, 2 * HID), CZ ** -0.5, 0.5)
    second_out = bell_draw(keys[8], (HID, CZ), HID ** -0.5, 0.25)
    head_weight = bell_draw(keys[9], (CZ, BINS), (CZ // 9) ** -0.5, 1.5)
    pae_bins = touch_ends(jax.random.randint(keys[10], (N, N), 0, BINS), jax.random.fold_in(keys[10], 1), 0, BINS - 1).astype(jnp.int32)
    chain_perm = draw_chain_perm(jax.random.fold_in(keys[14], 71), 0)
    resolved_counts = jax.vmap(lambda own: uneven_parts(own, N_COL, RES_DEV * N_COL, TILES_DEV, 2))(jax.random.split(keys[12], N_ROW)).reshape((N_ROW, N_COL)).astype(jnp.int32)
    tile_order = draw_tile_order(jax.random.fold_in(keys[14], 71), 0)
    return {"singles": singles, "pair_in": pair_in, "proj_weight": proj_weight, "gain_first": gain_first, "first_in": first_in, "first_out": first_out, "gain_second": gain_second, "second_in": second_in, "second_out": second_out, "head_weight": head_weight, "pae_bins": pae_bins, "chain_perm": chain_perm, "resolved_counts": resolved_counts, "tile_order": tile_order}


def contract(left_op, right_op, left_dim, right_dim):
    return lax.dot_general(left_op, right_op, (((left_dim,), (right_dim,)), ((), ())), preferred_element_type=jnp.float32)

def transition_forward(start_z, gain_vec, w_in, w_out):
    hidden_units = w_out.shape[0]
    average = lax.optimization_barrier(jnp.mean(start_z, axis=-1, keepdims=True))
    centred = start_z - average
    scaling = lax.rsqrt(lax.optimization_barrier(jnp.mean(centred * centred, axis=-1, keepdims=True)) + 1e-05)
    normed = centred * scaling
    inputs = (normed * gain_vec).astype(jnp.bfloat16)
    gate_up = jnp.dot(inputs, w_in, preferred_element_type=jnp.float32)
    gate_part = gate_up[:, :hidden_units]
    up_part = gate_up[:, hidden_units:]
    gate_sig = jax.nn.sigmoid(gate_part)
    hidden_act = (gate_part * gate_sig * up_part).astype(jnp.bfloat16)
    result = jnp.dot(hidden_act, w_out, preferred_element_type=jnp.float32)
    return (result, (normed, scaling, inputs, gate_part, up_part, gate_sig, hidden_act))

def transition_backward(saved, grad_out, gain_vec, w_in, w_out, with_weights):
    normed, scaling, inputs, gate_part, up_part, gate_sig, hidden_act = saved
    grad_hidden = contract(grad_out, w_out, 1, 1)
    grad_gate = grad_hidden * up_part * gate_sig * (1.0 + gate_part * (1.0 - gate_sig))
    grad_up = grad_hidden * gate_part * gate_sig
    grad_both = jnp.concatenate([grad_gate, grad_up], axis=1).astype(jnp.bfloat16)
    grad_normed = contract(grad_both, w_in, 1, 1) * gain_vec
    grad_field = scaling * (grad_normed - lax.optimization_barrier(jnp.mean(grad_normed, axis=-1, keepdims=True)) - normed * lax.optimization_barrier(jnp.mean(grad_normed * normed, axis=-1, keepdims=True)))
    if with_weights:
        return (grad_field, contract(inputs, grad_both, 0, 0), contract(hidden_act, grad_out, 0, 0))
    return (grad_field, None, None)

def head_step(rounded_z, targets, keep_mask, head_weight):
    logits = jnp.dot(rounded_z, head_weight, preferred_element_type=jnp.float32)
    exponent = jnp.exp(logits - lax.optimization_barrier(jnp.max(logits, axis=-1, keepdims=True)))
    probability = exponent / lax.optimization_barrier(jnp.sum(exponent, axis=-1, keepdims=True))
    onehot = (targets[:, None] == lax.broadcasted_iota(jnp.int32, logits.shape, 1)).astype(jnp.float32)
    grad_logits = ((probability - onehot) * keep_mask[:, None]).astype(jnp.bfloat16)
    return (contract(grad_logits, head_weight, 1, 1).astype(jnp.bfloat16), contract(rounded_z, grad_logits, 0, 0))

def second_step(pair_one, targets, live_mask, gain_second, second_in, second_out, head_weight):
    start_f = pair_one.astype(jnp.float32)
    delta, saved = transition_forward(start_f, gain_second, second_in, second_out)
    rounded_z = (start_f + live_mask[:, None] * delta).astype(jnp.bfloat16)
    grad_two, head_part = head_step(rounded_z, targets, jnp.ones_like(live_mask), head_weight)
    masked_out = jnp.where(live_mask[:, None] > 0, grad_two, jnp.zeros((), jnp.bfloat16))
    back_field, in_part, out_part = transition_backward(saved, masked_out, gain_second, second_in, second_out, True)
    return ((grad_two.astype(jnp.float32) + back_field).astype(jnp.bfloat16), in_part, out_part, head_part)

def reference(singles, pair_in, proj_weight, gain_first, first_in, first_out, gain_second, second_in, second_out, head_weight, pae_bins, chain_perm, resolved_counts, tile_order):
    projected = jnp.dot(singles, proj_weight, preferred_element_type=jnp.float32)
    left_part = projected[:, :CZ]
    right_round = lax.optimization_barrier(projected[:, CZ:].astype(jnp.bfloat16))
    right_part = right_round.astype(jnp.float32)
    order_grid = tile_order.reshape(N_ROW, N_COL, TILES_DEV)
    rank_grid = jnp.argsort(order_grid, axis=-1).astype(jnp.int32)
    tile_live = (rank_grid < resolved_counts[:, :, None]).reshape(N_ROW, N_COL, R_DEV, C_DEV // TILE)
    tile_live = tile_live.transpose(0, 2, 1, 3).reshape(N, N // TILE)
    pair_live = jnp.repeat(tile_live, TILE, axis=1).astype(jnp.float32)
    targets = pae_bins[chain_perm][:, chain_perm]
    band_rows = 16

    def band_step(running, band_index):
        first_row = band_index * band_rows
        pair_rows = lax.dynamic_slice_in_dim(pair_in, first_row, band_rows, 0).astype(jnp.float32)
        left_rows = lax.dynamic_slice_in_dim(left_part, first_row, band_rows, 0)
        start_z = (pair_rows + left_rows[:, None, :] + right_part[None, :, :]).reshape(band_rows * N, CZ)
        delta, saved_one = transition_forward(start_z, gain_first, first_in, first_out)
        pair_one = (start_z + delta).astype(jnp.bfloat16)
        band_targets = lax.dynamic_slice_in_dim(targets, first_row, band_rows, 0).reshape(band_rows * N)
        band_live = lax.dynamic_slice_in_dim(pair_live, first_row, band_rows, 0).reshape(band_rows * N)
        grad_one, in_part, out_part, head_part = second_step(pair_one, band_targets, band_live, gain_second, second_in, second_out, head_weight)
        back_field, unused_in, unused_out = transition_backward(saved_one, grad_one, gain_first, first_in, first_out, False)
        grad_zero = (grad_one.astype(jnp.float32) + back_field).reshape(band_rows, N, CZ)
        updated = (running[0] + lax.optimization_barrier(jnp.sum(grad_zero, axis=0)), running[1] + in_part, running[2] + out_part, running[3] + head_part)
        return (updated, (grad_zero.astype(jnp.bfloat16), lax.optimization_barrier(jnp.sum(grad_zero, axis=1))))
    initial = (jnp.zeros((N, CZ), jnp.float32), jnp.zeros((CZ, 2 * HID), jnp.float32), jnp.zeros((HID, CZ), jnp.float32), jnp.zeros((CZ, BINS), jnp.float32))
    totals, (pair_bands, left_bands) = lax.scan(band_step, initial, jnp.arange(N // band_rows, dtype=jnp.int32))
    token_grad = jnp.concatenate([left_bands.reshape(N, CZ), totals[0]], axis=1).astype(jnp.bfloat16)
    single_grad = contract(token_grad, proj_weight, 1, 1)
    return (pair_bands.reshape(N, N, CZ), single_grad, totals[1] / N, totals[2] / N, totals[3] / N)
```

```python
import functools
import jax
import jax.numpy as jnp
from jax import lax
from jax.experimental import pallas as pl
from jax.experimental.pallas import tpu as pltpu
from jax.sharding import PartitionSpec as P

TILE = 32
BLOCK_PAIRS = 512
CHUNK = 256
MESH = pl.DeviceIdType.MESH
BF = jnp.bfloat16
F32 = jnp.float32
VM = pl.BlockSpec(memory_space=pltpu.VMEM)
SM = pl.BlockSpec(memory_space=pltpu.SMEM)


def dot(left, right):
    return jnp.dot(left, right, preferred_element_type=F32)


def dot_rows(left, right):
    return lax.dot_general(left, right, (((0,), (0,)), ((), ())), preferred_element_type=F32)


def dot_lanes(left, right):
    return lax.dot_general(left, right, (((1,), (1,)), ((), ())), preferred_element_type=F32)


def prologue(
    n_row,
    n_col,
    singles,
    proj,
    bins,
    perm,
    counts,
    order,
    left_out,
    right_out,
    target_out,
    live_out,
    s_buf,
    w_buf,
    r_buf,
    s_send,
    s_recv,
    w_send,
    w_recv,
    r_send,
    r_recv,
    own_sem,
):
    row, col = lax.axis_index("row"), lax.axis_index("col")
    rows_dev = singles.shape[0]
    half = rows_dev // 2
    source_row = col // 2
    own_half = lax.rem(col, 2)
    own_right = source_row == row
    barrier = pltpu.get_barrier_semaphore()
    for k in range(1, n_col):
        peer = lax.rem(col + k, n_col)
        pl.semaphore_signal(barrier, inc=1, device_id=(row, peer), device_id_type=MESH)
        pl.semaphore_signal(barrier, inc=1, device_id=(source_row, peer), device_id_type=MESH)

    @pl.when(jnp.logical_not(own_right))
    def _():
        pl.semaphore_signal(barrier, inc=1, device_id=(source_row, col), device_id_type=MESH)

    pl.semaphore_wait(barrier, n_col - 1 + 2 * n_row - jnp.where(own_right, 1, 0))

    def s_copy(k):
        return pltpu.make_async_remote_copy(
            singles, s_buf.at[k], s_send.at[k], s_recv.at[k],
            device_id=(row, lax.rem(col + k, n_col)), device_id_type=MESH,
        )

    def w_copy(k):
        return pltpu.make_async_remote_copy(
            proj, w_buf.at[k], w_send.at[k], w_recv.at[k],
            device_id=(row, lax.rem(col + k, n_col)), device_id_type=MESH,
        )

    def r_copy(h, k):
        target = 2 * row + h
        slot = lax.rem(target - col + n_col, n_col)
        return pltpu.make_async_remote_copy(
            singles.at[pl.ds(h * half, half)], r_buf.at[slot], r_send.at[h, k], r_recv.at[slot],
            device_id=(lax.rem(row + k, n_row), target), device_id_type=MESH,
        )

    def own_copy(h):
        return pltpu.make_async_copy(singles.at[pl.ds(h * half, half)], r_buf.at[0], own_sem)

    def self_case(h):
        return jnp.logical_and(own_right, own_half == h)

    for k in range(1, n_col):
        w_copy(k).start()
        s_copy(k).start()
    for h in (0, 1):
        for k in range(1, n_row):
            r_copy(h, k).start()

        @pl.when(jnp.logical_not(self_case(h)))
        def _():
            r_copy(h, 0).start()

        @pl.when(self_case(h))
        def _():
            own_copy(h).start()

    group = perm.shape[1]
    count = counts[0, col]
    tiles = order.shape[1]
    hit = order[...] == lax.broadcasted_iota(jnp.int32, (tiles, tiles), 0)
    chosen = lax.broadcasted_iota(jnp.int32, (tiles, live_out.shape[1]), 0) < count
    live_out[...] = dot(
        jnp.where(hit, 1.0, 0.0).astype(BF), jnp.where(chosen, 1.0, 0.0).astype(BF)
    )
    place = lax.broadcasted_iota(jnp.int32, (group, group), 0)
    col_hit = jnp.where(perm[pl.ds(col, 1), :] - col * group == place, 1.0, 0.0).astype(BF)
    step_rows = BLOCK_PAIRS // group
    for h in (0, 1):
        index = 2 * row + h
        row_hit = jnp.where(perm[pl.ds(index, 1), :] - index * group == place, 1.0, 0.0).astype(BF)
        part = bins[pl.ds(h * group, group), :].astype(F32).astype(BF)
        wanted = dot(dot_rows(row_hit, part).astype(BF), col_hit)
        for b in range(group // step_rows):
            lanes = [wanted[b * step_rows + i : b * step_rows + i + 1, :] for i in range(step_rows)]
            target_out[h * (group // step_rows) + b] = jnp.concatenate(lanes, axis=1)

    width = proj.shape[1] // 2
    left_sum = dot(singles[...], proj[:, :width])
    for k in range(1, n_col):
        w_copy(k).wait()
        s_copy(k).wait()
        left_sum += dot(s_buf[k], w_buf[k, :, :width])
    left_out[...] = left_sum
    for h in (0, 1):
        for k in range(1, n_row):
            r_copy(h, k).wait_send()

        @pl.when(jnp.logical_not(self_case(h)))
        def _():
            r_copy(h, 0).wait_send()

        @pl.when(self_case(h))
        def _():
            own_copy(h).wait()

    def arrived(k):
        return pltpu.make_async_remote_copy(
            singles.at[pl.ds(0, half)], r_buf.at[k], r_send.at[0, 0], r_recv.at[k],
            device_id=(row, col), device_id_type=MESH,
        )

    @pl.when(jnp.logical_not(own_right))
    def _():
        arrived(0).wait_recv()

    right_sum = dot(r_buf[0], proj[:, width:])
    for k in range(1, n_col):
        arrived(k).wait_recv()
        right_sum += dot(r_buf[k], w_buf[k, :, width:])
    right_out[...] = right_sum.astype(BF).astype(F32)


def run_prologue(n_row, n_col, singles, proj, bins, perm, counts, order):
    rows_dev, chans = singles.shape
    wide = proj.shape[1]
    width = wide // 2
    cols_dev = bins.shape[1]
    tiles = order.shape[1]
    blocks = rows_dev * cols_dev // BLOCK_PAIRS
    dma = pltpu.SemaphoreType.DMA
    return pl.pallas_call(
        functools.partial(prologue, n_row, n_col),
        out_shape=[
            jax.ShapeDtypeStruct((rows_dev, width), F32),
            jax.ShapeDtypeStruct((cols_dev, width), F32),
            jax.ShapeDtypeStruct((blocks, 1, BLOCK_PAIRS), F32),
            jax.ShapeDtypeStruct((tiles, width), F32),
        ],
        in_specs=[VM, VM, VM, VM, SM, VM],
        out_specs=[VM] * 4,
        scratch_shapes=[
            pltpu.VMEM((n_col, rows_dev, chans), BF),
            pltpu.VMEM((n_col, chans, wide), BF),
            pltpu.VMEM((n_col, rows_dev // 2, chans), BF),
            dma((n_col,)), dma((n_col,)), dma((n_col,)), dma((n_col,)),
            dma((2, n_row)), dma((n_col,)), dma,
        ],
        compiler_params=pltpu.CompilerParams(collective_id=0, has_side_effects=True),
        name="prologue",
    )(singles, proj, bins, perm, counts, order)


def layer_norm(field):
    centred = field - jnp.mean(field, axis=-1, keepdims=True)
    scaling = lax.rsqrt(jnp.mean(centred * centred, axis=-1, keepdims=True) + 1e-05)
    return centred * scaling, scaling


def forward(inputs, w_in, w_out, a_ref, d_ref, h_ref):
    hidden = w_out.shape[0]
    total = None
    for c in range(0, hidden, CHUNK):
        here = pl.ds(c, CHUNK)
        gate = dot(inputs, w_in[:, here]).astype(BF)
        up = dot(inputs, w_in[:, pl.ds(hidden + c, CHUNK)]).astype(BF)
        low = gate * BF(0.5)
        twice = jnp.tanh(low) + BF(1)
        act = low * twice
        slope = act + (BF(0.5) * twice) * (BF(1) - act)
        value = act * up
        a_ref[:, here] = act
        d_ref[:, here] = up * slope
        if h_ref is not None:
            h_ref[:, here] = value
        part = dot(value, w_out[here, :])
        total = part if total is None else total + part
    return total


def backward(cot, w_in, w_out, a_ref, d_ref, b_ref):
    hidden = w_out.shape[0]
    total = None
    for c in range(0, hidden, CHUNK):
        here = pl.ds(c, CHUNK)
        there = pl.ds(hidden + c, CHUNK)
        grad_hidden = dot_lanes(cot, w_out[here, :]).astype(BF)
        grad_gate = grad_hidden * d_ref[:, here]
        grad_up = grad_hidden * a_ref[:, here]
        if b_ref is not None:
            b_ref[:, here] = grad_gate
            b_ref[:, there] = grad_up
        part = dot_lanes(grad_gate, w_in[:, here]) + dot_lanes(grad_up, w_in[:, there])
        total = part if total is None else total + part
    return total


def norm_backward(grad, gain, normed, scaling):
    grad = grad * gain
    return scaling * (
        grad
        - jnp.mean(grad, axis=-1, keepdims=True)
        - normed * jnp.mean(grad * normed, axis=-1, keepdims=True)
    )


def grid_step(
    pair, left, right, target, live, g1, w1, w1o, g2, w2, w2o, head,
    pair_grad, left_grad, right_grad, weight_out,
    a1, d1, a2, d2, h2, b2, n1, in_acc, out_acc, head_acc,
):
    pairs, width = pair.shape
    cols = right.shape[0]
    rows = pairs // cols
    step = pl.program_id(0)

    @pl.when(step == 0)
    def _():
        right_grad[...] = jnp.zeros_like(right_grad)
        in_acc[...] = jnp.zeros_like(in_acc)
        out_acc[...] = jnp.zeros_like(out_acc)
        head_acc[...] = jnp.zeros_like(head_acc)

    field = pair[...].astype(F32).reshape(rows, cols, width)
    field = (field + left[...][:, None, :] + right[...][None]).reshape(pairs, width)
    normed, s1 = layer_norm(field)
    n1[...] = normed
    delta = forward((normed * g1[...]).astype(BF), w1, w1o, a1, d1, None)
    second = (field + delta).astype(BF).astype(F32)
    normed2, s2 = layer_norm(second)
    inputs2 = (normed2 * g2[...]).astype(BF)
    delta2 = forward(inputs2, w2, w2o, a2, d2, h2)
    tiles = live.shape[0]
    mask = jnp.broadcast_to(live[...][:, None, :], (tiles, pairs // tiles, width))
    mask = mask.reshape(pairs, width)
    last = (second + mask * delta2).astype(BF)
    logits = dot_lanes(head[...], last)
    exponent = jnp.exp(logits - jnp.max(logits, axis=0, keepdims=True))
    prob = exponent / jnp.sum(exponent, axis=0, keepdims=True)
    bin_id = lax.broadcasted_iota(jnp.int32, logits.shape, 0).astype(F32)
    grad_logits = (prob - jnp.where(target[0] == bin_id, 1.0, 0.0)).astype(BF)
    head_acc[...] += dot(grad_logits, last)
    grad_two = dot_rows(grad_logits, head[...]).astype(BF).astype(F32)
    cot2 = jnp.where(mask > 0, grad_two, 0.0).astype(BF)
    normed_grad = backward(cot2, w2, w2o, a2, d2, b2)
    in_acc[...] += dot_rows(inputs2, b2[...])
    out_acc[...] += dot_rows(cot2, h2[...])
    grad_one = (grad_two + norm_backward(normed_grad, g2[...], normed2, s2)).astype(BF)
    normed_grad = backward(grad_one, w1, w1o, a1, d1, None)
    grad_zero = grad_one.astype(F32) + norm_backward(normed_grad, g1[...], n1[...], s1)
    pair_grad[...] = grad_zero.astype(BF)
    grid = grad_zero.reshape(rows, cols, width)
    right_grad[...] += jnp.sum(grid, axis=0)
    left_grad[...] = jnp.sum(grid, axis=1)

    @pl.when(step == pl.num_programs(0) - 1)
    def _():
        wide = in_acc.shape[1] // width
        for j in range(wide):
            weight_out[j * width : (j + 1) * width, :] = in_acc[:, j * width : (j + 1) * width].astype(BF)
        base = wide * width
        more = out_acc.shape[1] // width
        for j in range(more):
            block = out_acc[:, j * width : (j + 1) * width].T.astype(BF)
            weight_out[base + j * width : base + (j + 1) * width, :] = block
        base = base + more * width
        bins = head_acc.shape[0]
        weight_out[base : base + bins, :] = head_acc[...].astype(BF)
        rest = weight_out.shape[0] - base - bins
        weight_out[base + bins :, :] = jnp.zeros((rest, width), BF)


def run_grid(pay_rows, pair, left, right, target, live, g1, w1, w1o, g2, w2, w2o, head):
    pairs, width = pair.shape
    cols = right.shape[0]
    size = BLOCK_PAIRS
    steps = pairs // size
    rows = size // cols
    tiles = live.shape[0] // steps
    hidden = w1o.shape[0]
    bins = head.shape[0]

    def full(shape):
        return pl.BlockSpec(shape, lambda i: (0,) * len(shape))

    def part(shape):
        return pl.BlockSpec(shape, lambda i: (i,) + (0,) * (len(shape) - 1))

    return pl.pallas_call(
        grid_step,
        grid=(steps,),
        in_specs=[
            part((size, width)), part((rows, width)), full((cols, width)), part((1, 1, size)),
            part((tiles, width)), full((1, width)), full(w1.shape), full(w1o.shape),
            full((1, width)), full(w2.shape), full(w2o.shape), full(head.shape),
        ],
        out_specs=[
            part((size, width)), part((rows, width)), full((cols, width)), full((pay_rows, width)),
        ],
        out_shape=[
            jax.ShapeDtypeStruct((pairs, width), BF),
            jax.ShapeDtypeStruct((pairs // cols, width), F32),
            jax.ShapeDtypeStruct((cols, width), F32),
            jax.ShapeDtypeStruct((pay_rows, width), BF),
        ],
        scratch_shapes=[pltpu.VMEM((size, hidden), BF)] * 5
        + [
            pltpu.VMEM((size, 2 * hidden), BF),
            pltpu.VMEM((size, width), F32),
            pltpu.VMEM((width, 2 * hidden), F32),
            pltpu.VMEM((width, hidden), F32),
            pltpu.VMEM((bins, width), F32),
        ],
        compiler_params=pltpu.CompilerParams(dimension_semantics=("arbitrary",)),
        name="grid",
    )(pair, left, right, target, live, g1, w1, w1o, g2, w2, w2o, head)


def epilogue(
    n_row, n_col,
    weights, left_part, right_part, proj,
    in_out, out_out, head_out, single_out,
    in1, tok1, mid, tok_mid, in2, left2, right_all, left_all, gathered, final,
    send1, recv1, tsend1, trecv1, send2, recv2, lsend2, lrecv2, rsend, rrecv,
    send3, recv3, lsend3, lrecv3, send4, recv4, fsem,
):
    row, col = lax.axis_index("row"), lax.axis_index("col")
    width = weights.shape[1]
    share = weights.shape[0] // n_row
    small = mid.shape[0] // n_col
    tok = tok1.shape[1]
    target_row = col // 2
    self_case = target_row == row
    barrier = pltpu.get_barrier_semaphore()
    for k in range(1, n_row):
        peer = lax.rem(row + k, n_row)
        pl.semaphore_signal(barrier, inc=1, device_id=(peer, col), device_id_type=MESH)
        for h in (0, 1):
            pl.semaphore_signal(barrier, inc=1, device_id=(peer, 2 * row + h), device_id_type=MESH)
    for k in range(1, n_col):
        peer = lax.rem(col + k, n_col)
        pl.semaphore_signal(barrier, inc=1, device_id=(row, peer), device_id_type=MESH)
    for h in (0, 1):

        @pl.when(col != 2 * row + h)
        def _():
            pl.semaphore_signal(barrier, inc=1, device_id=(row, 2 * row + h), device_id_type=MESH)

    pl.semaphore_wait(barrier, n_row + n_col + n_col - 2 - jnp.where(self_case, 1, 0))

    def row_peer(k):
        return lax.rem(row + k, n_row)

    def col_peer(k):
        return lax.rem(col + k, n_col)

    def copy1(k):
        start = pl.multiple_of(row_peer(k) * share, share)
        return pltpu.make_async_remote_copy(
            weights.at[pl.ds(start, share)], in1.at[k], send1.at[k], recv1.at[k],
            device_id=(row_peer(k), col), device_id_type=MESH,
        )

    def tcopy1(k):
        start = pl.multiple_of(row_peer(k) * tok, tok)
        return pltpu.make_async_remote_copy(
            right_part.at[pl.ds(start, tok)], tok1.at[k], tsend1.at[k], trecv1.at[k],
            device_id=(row_peer(k), col), device_id_type=MESH,
        )

    def lcopy2(k):
        start = pl.multiple_of(col_peer(k) * tok, tok)
        return pltpu.make_async_remote_copy(
            left_part.at[pl.ds(start, tok)], left2.at[k], lsend2.at[k], lrecv2.at[k],
            device_id=(row, col_peer(k)), device_id_type=MESH,
        )

    for k in range(1, n_row):
        copy1(k).start()
        tcopy1(k).start()
    for k in range(1, n_col):
        lcopy2(k).start()

    own = right_part[pl.ds(pl.multiple_of(row * tok, tok), tok), :]
    for k in range(1, n_row):
        tcopy1(k).wait()
        own += tok1[k]
    tok_mid[...] = own
    slot = lax.rem(col, 2) * n_row + row

    def rcopy(k):
        return pltpu.make_async_remote_copy(
            tok_mid, right_all.at[slot], rsend.at[k], rrecv.at[slot],
            device_id=(target_row, col_peer(k)), device_id_type=MESH,
        )

    for k in range(1, n_col):
        rcopy(k).start()

    @pl.when(jnp.logical_not(self_case))
    def _():
        rcopy(0).start()

    own = left_part[pl.ds(pl.multiple_of(col * tok, tok), tok), :]
    for k in range(1, n_col):
        lcopy2(k).wait()
        own += left2[k]
    left_all[col] = own

    def lcopy3(k):
        return pltpu.make_async_remote_copy(
            left_all.at[col], left_all.at[col], lsend3.at[k], lrecv3.at[col],
            device_id=(row, col_peer(k)), device_id_type=MESH,
        )

    for k in range(1, n_col):
        lcopy3(k).start()

    total = weights[pl.ds(pl.multiple_of(row * share, share), share), :].astype(F32)
    for k in range(1, n_row):
        copy1(k).wait()
        total += in1[k].astype(F32)
    mid[:share, :] = total.astype(BF)
    mid[share:, :] = jnp.zeros((mid.shape[0] - share, width), BF)

    def copy2(k):
        start = pl.multiple_of(col_peer(k) * small, small)
        return pltpu.make_async_remote_copy(
            mid.at[pl.ds(start, small)], in2.at[k], send2.at[k], recv2.at[k],
            device_id=(row, col_peer(k)), device_id_type=MESH,
        )

    for k in range(1, n_col):
        copy2(k).start()
    total = mid[pl.ds(pl.multiple_of(col * small, small), small), :].astype(F32)
    for k in range(1, n_col):
        copy2(k).wait()
        total += in2[k].astype(F32)
    mine = pl.ds(pl.multiple_of(col * small, small), small)
    gathered[mine, :] = total.astype(BF)

    def copy3(k):
        return pltpu.make_async_remote_copy(
            gathered.at[mine], gathered.at[mine], send3.at[k], recv3.at[col],
            device_id=(row, col_peer(k)), device_id_type=MESH,
        )

    def came3(j):
        spot = pl.ds(pl.multiple_of(j * small, small), small)
        return pltpu.make_async_remote_copy(
            gathered.at[spot], gathered.at[spot], send3.at[0], recv3.at[j],
            device_id=(row, j), device_id_type=MESH,
        )

    for k in range(1, n_col):
        copy3(k).start()
    for k in range(1, n_col):
        came3(col_peer(k)).wait_recv()
    for k in range(1, n_col):
        copy3(k).wait_send()

    band = pl.ds(pl.multiple_of(row * share, share), share)

    def copy4(k):
        return pltpu.make_async_remote_copy(
            gathered.at[pl.ds(0, share)], final.at[band], send4.at[k], recv4.at[row],
            device_id=(row_peer(k), col), device_id_type=MESH,
        )

    def came4(j):
        spot = pl.ds(pl.multiple_of(j * share, share), share)
        return pltpu.make_async_remote_copy(
            gathered.at[pl.ds(0, share)], final.at[spot], send4.at[0], recv4.at[j],
            device_id=(j, col), device_id_type=MESH,
        )

    for k in range(1, n_row):
        copy4(k).start()
    own_copy = pltpu.make_async_copy(gathered.at[pl.ds(0, share)], final.at[band], fsem)
    own_copy.start()

    def lcame(j):
        return pltpu.make_async_remote_copy(
            left_all.at[j], left_all.at[j], lsend3.at[0], lrecv3.at[j],
            device_id=(row, j), device_id_type=MESH,
        )

    def rcame(j):
        return pltpu.make_async_remote_copy(
            tok_mid, right_all.at[j], rsend.at[0], rrecv.at[j],
            device_id=(row, col), device_id_type=MESH,
        )

    for k in range(1, n_col):
        lcame(col_peer(k)).wait_recv()
        lcopy3(k).wait_send()
        rcopy(k).wait_send()

    @pl.when(jnp.logical_not(self_case))
    def _():
        rcopy(0).wait_send()

    for k in range(1, n_col):
        rcame(lax.rem(slot + k, n_col)).wait_recv()

    @pl.when(jnp.logical_not(self_case))
    def _():
        rcame(slot).wait_recv()

    @pl.when(self_case)
    def _():
        right_all[slot] = tok_mid[...]

    tokens = n_col * tok
    left_tok = left_all[...].reshape(tokens, width).astype(BF)
    right_tok = right_all[...].reshape(tokens, width).astype(BF)
    single_out[...] = dot_lanes(left_tok, proj[:, :width]) + dot_lanes(right_tok, proj[:, width:])

    own_copy.wait()
    for k in range(1, n_row):
        came4(row_peer(k)).wait_recv()
    for k in range(1, n_row):
        copy4(k).wait_send()
    scale = 1.0 / (n_row * tokens)
    wide = in_out.shape[1] // width
    for j in range(wide):
        block = final[j * width : (j + 1) * width, :].astype(F32) * scale
        in_out[:, j * width : (j + 1) * width] = block
    base = wide * width
    hidden = out_out.shape[0]
    out_out[...] = final[base : base + hidden, :].astype(F32) * scale
    bins = head_out.shape[0]
    head_out[...] = final[base + hidden : base + hidden + bins, :].astype(F32) * scale


def run_epilogue(n_row, n_col, hidden, bins, weights, left_part, right_part, proj):
    width = weights.shape[1]
    pay = weights.shape[0]
    share = pay // n_row
    rows_dev = left_part.shape[0]
    tok = rows_dev // n_col
    small = -(-share // (16 * n_col)) * 16
    dma = pltpu.SemaphoreType.DMA
    sems = [
        n_row, n_row, n_row, n_row, n_col, n_col, n_col, n_col, n_col, n_col,
        n_col, n_col, n_col, n_col, n_row, n_row,
    ]
    return pl.pallas_call(
        functools.partial(epilogue, n_row, n_col),
        out_shape=[
            jax.ShapeDtypeStruct((width, 2 * hidden), F32),
            jax.ShapeDtypeStruct((hidden, width), F32),
            jax.ShapeDtypeStruct((bins, width), F32),
            jax.ShapeDtypeStruct((rows_dev, proj.shape[0]), F32),
        ],
        in_specs=[VM] * 4,
        out_specs=[VM] * 4,
        scratch_shapes=[
            pltpu.VMEM((n_row, share, width), BF),
            pltpu.VMEM((n_row, tok, width), F32),
            pltpu.VMEM((small * n_col, width), BF),
            pltpu.VMEM((tok, width), F32),
            pltpu.VMEM((n_col, small, width), BF),
            pltpu.VMEM((n_col, tok, width), F32),
            pltpu.VMEM((n_col, tok, width), F32),
            pltpu.VMEM((n_col, tok, width), F32),
            pltpu.VMEM((small * n_col, width), BF),
            pltpu.VMEM((pay, width), BF),
        ]
        + [dma((n,)) for n in sems]
        + [dma],
        compiler_params=pltpu.CompilerParams(collective_id=1, has_side_effects=True),
        name="epilogue",
    )(weights, left_part, right_part, proj)


def local(
    n_row, n_col,
    singles, pair_in, proj_weight, gain_first, first_in, first_out, gain_second, second_in,
    second_out, head_weight, pae_bins, chain_perm, resolved_counts, tile_order,
):
    rows_dev, cols_dev, width = pair_in.shape
    hidden = first_out.shape[0]
    bins = head_weight.shape[1]
    left, right, target, live = run_prologue(
        n_row, n_col, singles, proj_weight, pae_bins, chain_perm.reshape(-1, cols_dev),
        resolved_counts, tile_order,
    )
    need = 3 * hidden + bins
    pay = -(-need // (16 * n_row)) * 16 * n_row
    pair_grad, left_part, right_part, weights = run_grid(
        pay, pair_in.reshape(rows_dev * cols_dev, width), left, right, target, live,
        gain_first.reshape(1, width), first_in, first_out,
        gain_second.reshape(1, width), second_in, second_out, head_weight.T,
    )
    in_grad, out_grad, head_grad, single_grad = run_epilogue(
        n_row, n_col, hidden, bins, weights, left_part, right_part, proj_weight
    )
    return (
        pair_grad.reshape(rows_dev, cols_dev, width), single_grad, in_grad, out_grad, head_grad.T,
    )


def solution(mesh):
    in_specs = (
        P("row", "col"), P("row", "col", None), P("col", None), P(), P(), P(), P(), P(), P(), P(),
        P("row", "col"), P(), P("row", None), P("row", "col"),
    )
    out_specs = (P("row", "col", None), P("row", "col"), P(), P(), P())
    body = functools.partial(local, mesh.shape["row"], mesh.shape["col"])
    return jax.shard_map(body, mesh=mesh, in_specs=in_specs, out_specs=out_specs, check_vma=False)
```

```python
import functools
import jax
import jax.numpy as jnp
from jax import lax
from jax.experimental import pallas as pl
from jax.experimental.pallas import tpu as pltpu
from jax.sharding import PartitionSpec as P

TILE = 32
BLOCK_PAIRS = 512
CHUNK = 256
MESH = pl.DeviceIdType.MESH
BF = jnp.bfloat16
F32 = jnp.float32
VM = pl.BlockSpec(memory_space=pltpu.VMEM)
SM = pl.BlockSpec(memory_space=pltpu.SMEM)


def dot(left, right):
    return jnp.dot(left, right, preferred_element_type=F32)


def dot_rows(left, right):
    return lax.dot_general(left, right, (((0,), (0,)), ((), ())), preferred_element_type=F32)


def dot_lanes(left, right):
    return lax.dot_general(left, right, (((1,), (1,)), ((), ())), preferred_element_type=F32)


def prologue(
    n_row,
    n_col,
    singles,
    proj,
    bins,
    perm,
    counts,
    order,
    left_out,
    right_out,
    target_out,
    live_out,
    s_buf,
    w_buf,
    r_buf,
    r_full,
    s_send,
    s_recv,
    w_send,
    w_recv,
    r_send,
    r_recv,
):
    row, col = lax.axis_index("row"), lax.axis_index("col")
    chans = singles.shape[0]
    room = s_buf.shape[0] // n_col
    source_row = col // 2
    own_right = source_row == row
    s_buf[...] = jnp.zeros_like(s_buf)
    w_buf[...] = jnp.zeros_like(w_buf)
    r_buf[...] = jnp.zeros_like(r_buf)
    barrier = pltpu.get_barrier_semaphore()
    for k in range(1, n_col):
        peer = lax.rem(col + k, n_col)
        pl.semaphore_signal(barrier, inc=1, device_id=(row, peer), device_id_type=MESH)
        pl.semaphore_signal(barrier, inc=1, device_id=(source_row, peer), device_id_type=MESH)

    @pl.when(jnp.logical_not(own_right))
    def _():
        pl.semaphore_signal(barrier, inc=1, device_id=(source_row, col), device_id_type=MESH)

    pl.semaphore_wait(barrier, n_col - 1 + 2 * n_row - jnp.where(own_right, 1, 0))

    def spot(k):
        return pl.ds(k * room, chans)

    def s_copy(k):
        return pltpu.make_async_remote_copy(
            singles, s_buf.at[spot(k)], s_send.at[k], s_recv.at[k],
            device_id=(row, lax.rem(col + k, n_col)), device_id_type=MESH,
        )

    def w_copy(k):
        return pltpu.make_async_remote_copy(
            proj, w_buf.at[spot(k)], w_send.at[k], w_recv.at[k],
            device_id=(row, lax.rem(col + k, n_col)), device_id_type=MESH,
        )

    def r_copy(h, k):
        target = 2 * row + h
        slot = lax.rem(target - col + n_col, n_col)
        place = pl.ds(pl.multiple_of(slot * room, room), chans)
        return pltpu.make_async_remote_copy(
            singles, r_buf.at[place], r_send.at[h, k], r_recv.at[slot],
            device_id=(lax.rem(row + k, n_row), target), device_id_type=MESH,
        )

    def other(h):
        return col != 2 * row + h

    for k in range(1, n_col):
        w_copy(k).start()
        s_copy(k).start()
    for h in (0, 1):
        for k in range(1, n_row):
            r_copy(h, k).start()

        @pl.when(other(h))
        def _():
            r_copy(h, 0).start()

    s_buf[spot(0), :] = singles[...]
    w_buf[spot(0), :] = proj[...]

    @pl.when(own_right)
    def _():
        r_buf[spot(0), :] = singles[...]

    group = bins.shape[0]
    count = counts[0, col]
    tiles = order.shape[1]
    hit = order[...] == lax.broadcasted_iota(jnp.int32, (tiles, tiles), 0)
    chosen = lax.broadcasted_iota(jnp.int32, (tiles, live_out.shape[1]), 0) < count
    live_out[...] = dot(
        jnp.where(hit, 1.0, 0.0).astype(BF), jnp.where(chosen, 1.0, 0.0).astype(BF)
    )
    place = lax.broadcasted_iota(jnp.int32, (group, group), 0)
    pair_of = perm[pl.ds(source_row, 1), :]
    mine = jnp.where(lax.rem(col, 2) == 0, pair_of[:, :group], pair_of[:, group:])
    col_hit = jnp.where(mine - col * group == place, 1.0, 0.0).astype(BF)
    pair_of = perm[pl.ds(row, 1), :]
    step_rows = BLOCK_PAIRS // group
    for h in (0, 1):
        mine = pair_of[:, h * group : (h + 1) * group] - (2 * row + h) * group
        row_hit = jnp.where(mine == place, 1.0, 0.0).astype(BF)
        part = bins[:, h * group : (h + 1) * group].astype(F32).astype(BF)
        wanted = dot_rows(row_hit, dot_rows(part, col_hit).astype(BF))
        for b in range(group // step_rows):
            lanes = [wanted[b * step_rows + i : b * step_rows + i + 1, :] for i in range(step_rows)]
            target_out[h * (group // step_rows) + b] = jnp.concatenate(lanes, axis=1)

    width = proj.shape[1] // 2
    for k in range(1, n_col):
        w_copy(k).wait()
        s_copy(k).wait()
    left_out[...] = dot_rows(s_buf[...], w_buf[:, :width])

    def arrived(k):
        return pltpu.make_async_remote_copy(
            singles, r_buf.at[spot(k)], r_send.at[0, 0], r_recv.at[k],
            device_id=(row, col), device_id_type=MESH,
        )

    @pl.when(jnp.logical_not(own_right))
    def _():
        arrived(0).wait_recv()

    for k in range(1, n_col):
        arrived(k).wait_recv()
    r_full[...] = dot_rows(r_buf[...], w_buf[:, width:]).astype(BF).astype(F32)
    half = right_out.shape[0]
    right_out[...] = r_full[pl.ds(pl.multiple_of(lax.rem(col, 2) * half, half), half), :]
    for h in (0, 1):
        for k in range(1, n_row):
            r_copy(h, k).wait_send()

        @pl.when(other(h))
        def _():
            r_copy(h, 0).wait_send()


def run_prologue(n_row, n_col, singles, proj, bins, perm, counts, order):
    chans, rows_dev = singles.shape
    wide = proj.shape[1]
    width = wide // 2
    cols_dev = bins.shape[0]
    tiles = order.shape[1]
    blocks = rows_dev * cols_dev // BLOCK_PAIRS
    room = -(-chans // 16) * 16
    dma = pltpu.SemaphoreType.DMA
    return pl.pallas_call(
        functools.partial(prologue, n_row, n_col),
        out_shape=[
            jax.ShapeDtypeStruct((rows_dev, width), F32),
            jax.ShapeDtypeStruct((cols_dev, width), F32),
            jax.ShapeDtypeStruct((blocks, 1, BLOCK_PAIRS), F32),
            jax.ShapeDtypeStruct((tiles, width), F32),
        ],
        in_specs=[VM, VM, VM, VM, SM, VM],
        out_specs=[VM] * 4,
        scratch_shapes=[
            pltpu.VMEM((n_col * room, rows_dev), BF),
            pltpu.VMEM((n_col * room, wide), BF),
            pltpu.VMEM((n_col * room, rows_dev), BF),
            pltpu.VMEM((rows_dev, width), F32),
            dma((n_col,)), dma((n_col,)), dma((n_col,)), dma((n_col,)),
            dma((2, n_row)), dma((n_col,)),
        ],
        compiler_params=pltpu.CompilerParams(collective_id=0, has_side_effects=True),
        name="prologue",
    )(singles, proj, bins, perm, counts, order)


def layer_norm(field):
    centred = field - jnp.mean(field, axis=-1, keepdims=True)
    scaling = lax.rsqrt(jnp.mean(centred * centred, axis=-1, keepdims=True) + 1e-05)
    return centred * scaling, scaling


def forward(inputs, w_in, w_out, a_ref, d_ref, h_ref):
    hidden = w_out.shape[0]
    total = None
    for c in range(0, hidden, CHUNK):
        here = pl.ds(c, CHUNK)
        gate = dot(inputs, w_in[:, here]).astype(BF)
        up = dot(inputs, w_in[:, pl.ds(hidden + c, CHUNK)]).astype(BF)
        low = gate * BF(0.5)
        twice = jnp.tanh(low) + BF(1)
        act = low * twice
        slope = act + (BF(0.5) * twice) * (BF(1) - act)
        value = act * up
        a_ref[:, here] = act
        d_ref[:, here] = up * slope
        if h_ref is not None:
            h_ref[:, here] = value
        part = dot(value, w_out[here, :])
        total = part if total is None else total + part
    return total


def backward(cot, w_in, w_out, a_ref, d_ref, b_ref):
    hidden = w_out.shape[0]
    total = None
    for c in range(0, hidden, CHUNK):
        here = pl.ds(c, CHUNK)
        there = pl.ds(hidden + c, CHUNK)
        grad_hidden = dot_lanes(cot, w_out[here, :]).astype(BF)
        grad_gate = grad_hidden * d_ref[:, here]
        grad_up = grad_hidden * a_ref[:, here]
        if b_ref is not None:
            b_ref[:, here] = grad_gate
            b_ref[:, there] = grad_up
        part = dot_lanes(grad_gate, w_in[:, here]) + dot_lanes(grad_up, w_in[:, there])
        total = part if total is None else total + part
    return total


def norm_backward(grad, gain, normed, scaling):
    grad = grad * gain
    return scaling * (
        grad
        - jnp.mean(grad, axis=-1, keepdims=True)
        - normed * jnp.mean(grad * normed, axis=-1, keepdims=True)
    )


def grid_step(
    pair, left, right, target, live, g1, w1, w1o, g2, w2, w2o, head,
    pair_grad, left_grad, right_grad, weight_out,
    a1, d1, a2, d2, h2, b2, n1, in_acc, out_acc, head_acc,
):
    pairs, width = pair.shape
    cols = right.shape[0]
    rows = pairs // cols
    step = pl.program_id(0)

    @pl.when(step == 0)
    def _():
        right_grad[...] = jnp.zeros_like(right_grad)
        in_acc[...] = jnp.zeros_like(in_acc)
        out_acc[...] = jnp.zeros_like(out_acc)
        head_acc[...] = jnp.zeros_like(head_acc)

    field = pair[...].astype(F32).reshape(rows, cols, width)
    field = (field + left[...][:, None, :] + right[...][None]).reshape(pairs, width)
    normed, s1 = layer_norm(field)
    n1[...] = normed
    delta = forward((normed * g1[...]).astype(BF), w1, w1o, a1, d1, None)
    second = (field + delta).astype(BF).astype(F32)
    normed2, s2 = layer_norm(second)
    inputs2 = (normed2 * g2[...]).astype(BF)
    delta2 = forward(inputs2, w2, w2o, a2, d2, h2)
    tiles = live.shape[0]
    mask = jnp.broadcast_to(live[...][:, None, :], (tiles, pairs // tiles, width))
    mask = mask.reshape(pairs, width)
    last = (second + mask * delta2).astype(BF)
    logits = dot_lanes(head[...], last)
    exponent = jnp.exp(logits - jnp.max(logits, axis=0, keepdims=True))
    prob = exponent / jnp.sum(exponent, axis=0, keepdims=True)
    bin_id = lax.broadcasted_iota(jnp.int32, logits.shape, 0).astype(F32)
    grad_logits = (prob - jnp.where(target[0] == bin_id, 1.0, 0.0)).astype(BF)
    head_acc[...] += dot(grad_logits, last)
    grad_two = dot_rows(grad_logits, head[...]).astype(BF).astype(F32)
    cot2 = jnp.where(mask > 0, grad_two, 0.0).astype(BF)
    normed_grad = backward(cot2, w2, w2o, a2, d2, b2)
    in_acc[...] += dot_rows(inputs2, b2[...])
    out_acc[...] += dot_rows(cot2, h2[...])
    grad_one = (grad_two + norm_backward(normed_grad, g2[...], normed2, s2)).astype(BF)
    normed_grad = backward(grad_one, w1, w1o, a1, d1, None)
    grad_zero = grad_one.astype(F32) + norm_backward(normed_grad, g1[...], n1[...], s1)
    pair_grad[...] = grad_zero.astype(BF)
    grid = grad_zero.reshape(rows, cols, width)
    right_grad[...] += jnp.sum(grid, axis=0)
    left_grad[...] = jnp.sum(grid, axis=1)

    @pl.when(step == pl.num_programs(0) - 1)
    def _():
        wide = in_acc.shape[1] // width
        for j in range(wide):
            weight_out[j * width : (j + 1) * width, :] = in_acc[:, j * width : (j + 1) * width].astype(BF)
        base = wide * width
        more = out_acc.shape[1] // width
        for j in range(more):
            block = out_acc[:, j * width : (j + 1) * width].T.astype(BF)
            weight_out[base + j * width : base + (j + 1) * width, :] = block
        base = base + more * width
        bins = head_acc.shape[0]
        weight_out[base : base + bins, :] = head_acc[...].astype(BF)
        rest = weight_out.shape[0] - base - bins
        weight_out[base + bins :, :] = jnp.zeros((rest, width), BF)


def run_grid(pay_rows, pair, left, right, target, live, g1, w1, w1o, g2, w2, w2o, head):
    pairs, width = pair.shape
    cols = right.shape[0]
    size = BLOCK_PAIRS
    steps = pairs // size
    rows = size // cols
    tiles = live.shape[0] // steps
    hidden = w1o.shape[0]
    bins = head.shape[0]

    def full(shape):
        return pl.BlockSpec(shape, lambda i: (0,) * len(shape))

    def part(shape):
        return pl.BlockSpec(shape, lambda i: (i,) + (0,) * (len(shape) - 1))

    return pl.pallas_call(
        grid_step,
        grid=(steps,),
        in_specs=[
            part((size, width)), part((rows, width)), full((cols, width)), part((1, 1, size)),
            part((tiles, width)), full((1, width)), full(w1.shape), full(w1o.shape),
            full((1, width)), full(w2.shape), full(w2o.shape), full(head.shape),
        ],
        out_specs=[
            part((size, width)), part((rows, width)), full((cols, width)), full((pay_rows, width)),
        ],
        out_shape=[
            jax.ShapeDtypeStruct((pairs, width), BF),
            jax.ShapeDtypeStruct((pairs // cols, width), F32),
            jax.ShapeDtypeStruct((cols, width), F32),
            jax.ShapeDtypeStruct((pay_rows, width), BF),
        ],
        scratch_shapes=[pltpu.VMEM((size, hidden), BF)] * 5
        + [
            pltpu.VMEM((size, 2 * hidden), BF),
            pltpu.VMEM((size, width), F32),
            pltpu.VMEM((width, 2 * hidden), F32),
            pltpu.VMEM((width, hidden), F32),
            pltpu.VMEM((bins, width), F32),
        ],
        compiler_params=pltpu.CompilerParams(dimension_semantics=("arbitrary",)),
        name="grid",
    )(pair, left, right, target, live, g1, w1, w1o, g2, w2, w2o, head)


def epilogue(
    n_row, n_col,
    weights, left_part, right_part, proj,
    final, single_out,
    in1, tok1, mid, tok_mid, in2, left2, right_all, left_all, gathered,
    send1, recv1, tsend1, trecv1, send2, recv2, lsend2, lrecv2, rsend, rrecv,
    send3, recv3, lsend3, lrecv3, send4, recv4, fsem,
):
    row, col = lax.axis_index("row"), lax.axis_index("col")
    width = weights.shape[1]
    share = weights.shape[0] // n_row
    small = mid.shape[0] // n_col
    tok = tok1.shape[1]
    target_row = col // 2
    self_case = target_row == row
    barrier = pltpu.get_barrier_semaphore()
    for k in range(1, n_row):
        peer = lax.rem(row + k, n_row)
        pl.semaphore_signal(barrier, inc=1, device_id=(peer, col), device_id_type=MESH)
        for h in (0, 1):
            pl.semaphore_signal(barrier, inc=1, device_id=(peer, 2 * row + h), device_id_type=MESH)
    for k in range(1, n_col):
        peer = lax.rem(col + k, n_col)
        pl.semaphore_signal(barrier, inc=1, device_id=(row, peer), device_id_type=MESH)
    for h in (0, 1):

        @pl.when(col != 2 * row + h)
        def _():
            pl.semaphore_signal(barrier, inc=1, device_id=(row, 2 * row + h), device_id_type=MESH)

    pl.semaphore_wait(barrier, n_row + n_col + n_col - 2 - jnp.where(self_case, 1, 0))

    def row_peer(k):
        return lax.rem(row + k, n_row)

    def col_peer(k):
        return lax.rem(col + k, n_col)

    def copy1(k):
        start = pl.multiple_of(row_peer(k) * share, share)
        return pltpu.make_async_remote_copy(
            weights.at[pl.ds(start, share)], in1.at[k], send1.at[k], recv1.at[k],
            device_id=(row_peer(k), col), device_id_type=MESH,
        )

    def tcopy1(k):
        start = pl.multiple_of(row_peer(k) * tok, tok)
        return pltpu.make_async_remote_copy(
            right_part.at[pl.ds(start, tok)], tok1.at[k], tsend1.at[k], trecv1.at[k],
            device_id=(row_peer(k), col), device_id_type=MESH,
        )

    def lcopy2(k):
        start = pl.multiple_of(col_peer(k) * tok, tok)
        return pltpu.make_async_remote_copy(
            left_part.at[pl.ds(start, tok)], left2.at[k], lsend2.at[k], lrecv2.at[k],
            device_id=(row, col_peer(k)), device_id_type=MESH,
        )

    for k in range(1, n_row):
        copy1(k).start()
        tcopy1(k).start()
    for k in range(1, n_col):
        lcopy2(k).start()

    own = right_part[pl.ds(pl.multiple_of(row * tok, tok), tok), :]
    for k in range(1, n_row):
        tcopy1(k).wait()
        own += tok1[k]
    tok_mid[...] = own
    slot = lax.rem(col, 2) * n_row + row

    def rcopy(k):
        return pltpu.make_async_remote_copy(
            tok_mid, right_all.at[slot], rsend.at[k], rrecv.at[slot],
            device_id=(target_row, col_peer(k)), device_id_type=MESH,
        )

    for k in range(1, n_col):
        rcopy(k).start()

    @pl.when(jnp.logical_not(self_case))
    def _():
        rcopy(0).start()

    own = left_part[pl.ds(pl.multiple_of(col * tok, tok), tok), :]
    for k in range(1, n_col):
        lcopy2(k).wait()
        own += left2[k]
    left_all[col] = own

    def lcopy3(k):
        return pltpu.make_async_remote_copy(
            left_all.at[col], left_all.at[col], lsend3.at[k], lrecv3.at[col],
            device_id=(row, col_peer(k)), device_id_type=MESH,
        )

    for k in range(1, n_col):
        lcopy3(k).start()

    total = weights[pl.ds(pl.multiple_of(row * share, share), share), :].astype(F32)
    for k in range(1, n_row):
        copy1(k).wait()
        total += in1[k].astype(F32)
    mid[:share, :] = total.astype(BF)
    mid[share:, :] = jnp.zeros((mid.shape[0] - share, width), BF)

    def copy2(k):
        start = pl.multiple_of(col_peer(k) * small, small)
        return pltpu.make_async_remote_copy(
            mid.at[pl.ds(start, small)], in2.at[k], send2.at[k], recv2.at[k],
            device_id=(row, col_peer(k)), device_id_type=MESH,
        )

    for k in range(1, n_col):
        copy2(k).start()
    total = mid[pl.ds(pl.multiple_of(col * small, small), small), :].astype(F32)
    for k in range(1, n_col):
        copy2(k).wait()
        total += in2[k].astype(F32)
    mine = pl.ds(pl.multiple_of(col * small, small), small)
    gathered[mine, :] = total.astype(BF)

    def copy3(k):
        return pltpu.make_async_remote_copy(
            gathered.at[mine], gathered.at[mine], send3.at[k], recv3.at[col],
            device_id=(row, col_peer(k)), device_id_type=MESH,
        )

    def came3(j):
        spot = pl.ds(pl.multiple_of(j * small, small), small)
        return pltpu.make_async_remote_copy(
            gathered.at[spot], gathered.at[spot], send3.at[0], recv3.at[j],
            device_id=(row, j), device_id_type=MESH,
        )

    for k in range(1, n_col):
        copy3(k).start()
    for k in range(1, n_col):
        came3(col_peer(k)).wait_recv()
    for k in range(1, n_col):
        copy3(k).wait_send()

    band = pl.ds(pl.multiple_of(row * share, share), share)

    def copy4(k):
        return pltpu.make_async_remote_copy(
            gathered.at[pl.ds(0, share)], final.at[band], send4.at[k], recv4.at[row],
            device_id=(row_peer(k), col), device_id_type=MESH,
        )

    def came4(j):
        spot = pl.ds(pl.multiple_of(j * share, share), share)
        return pltpu.make_async_remote_copy(
            gathered.at[pl.ds(0, share)], final.at[spot], send4.at[0], recv4.at[j],
            device_id=(j, col), device_id_type=MESH,
        )

    for k in range(1, n_row):
        copy4(k).start()
    own_copy = pltpu.make_async_copy(gathered.at[pl.ds(0, share)], final.at[band], fsem)
    own_copy.start()

    def lcame(j):
        return pltpu.make_async_remote_copy(
            left_all.at[j], left_all.at[j], lsend3.at[0], lrecv3.at[j],
            device_id=(row, j), device_id_type=MESH,
        )

    def rcame(j):
        return pltpu.make_async_remote_copy(
            tok_mid, right_all.at[j], rsend.at[0], rrecv.at[j],
            device_id=(row, col), device_id_type=MESH,
        )

    for k in range(1, n_col):
        lcame(col_peer(k)).wait_recv()
        lcopy3(k).wait_send()
        rcopy(k).wait_send()

    @pl.when(jnp.logical_not(self_case))
    def _():
        rcopy(0).wait_send()

    for k in range(1, n_col):
        rcame(lax.rem(slot + k, n_col)).wait_recv()

    @pl.when(jnp.logical_not(self_case))
    def _():
        rcame(slot).wait_recv()

    @pl.when(self_case)
    def _():
        right_all[slot] = tok_mid[...]

    tokens = n_col * tok
    left_tok = left_all[...].reshape(tokens, width).astype(BF)
    right_tok = right_all[...].reshape(tokens, width).astype(BF)
    single_out[...] = dot_lanes(proj[:, :width], left_tok) + dot_lanes(proj[:, width:], right_tok)

    own_copy.wait()
    for k in range(1, n_row):
        came4(row_peer(k)).wait_recv()
    for k in range(1, n_row):
        copy4(k).wait_send()


def run_epilogue(n_row, n_col, weights, left_part, right_part, proj):
    width = weights.shape[1]
    pay = weights.shape[0]
    share = pay // n_row
    rows_dev = left_part.shape[0]
    tok = rows_dev // n_col
    small = -(-share // (16 * n_col)) * 16
    dma = pltpu.SemaphoreType.DMA
    sems = [
        n_row, n_row, n_row, n_row, n_col, n_col, n_col, n_col, n_col, n_col,
        n_col, n_col, n_col, n_col, n_row, n_row,
    ]
    return pl.pallas_call(
        functools.partial(epilogue, n_row, n_col),
        out_shape=[
            jax.ShapeDtypeStruct((pay, width), BF),
            jax.ShapeDtypeStruct((proj.shape[0], rows_dev), F32),
        ],
        in_specs=[VM] * 4,
        out_specs=[VM] * 2,
        scratch_shapes=[
            pltpu.VMEM((n_row, share, width), BF),
            pltpu.VMEM((n_row, tok, width), F32),
            pltpu.VMEM((small * n_col, width), BF),
            pltpu.VMEM((tok, width), F32),
            pltpu.VMEM((n_col, small, width), BF),
            pltpu.VMEM((n_col, tok, width), F32),
            pltpu.VMEM((n_col, tok, width), F32),
            pltpu.VMEM((n_col, tok, width), F32),
            pltpu.VMEM((small * n_col, width), BF),
        ]
        + [dma((n,)) for n in sems]
        + [dma],
        compiler_params=pltpu.CompilerParams(collective_id=1, has_side_effects=True),
        name="epilogue",
    )(weights, left_part, right_part, proj)


def finish(scale, sums, single, in_out, out_out, head_out, single_out):
    width = sums.shape[1]
    wide = in_out.shape[1] // width
    for j in range(wide):
        block = sums[j * width : (j + 1) * width, :].astype(F32) * scale
        in_out[:, j * width : (j + 1) * width] = block
    base = wide * width
    hidden = out_out.shape[0]
    out_out[...] = sums[base : base + hidden, :].astype(F32) * scale
    bins = head_out.shape[0]
    head_out[...] = sums[base + hidden : base + hidden + bins, :].astype(F32) * scale
    single_out[...] = single[...]


def run_finish(tokens, hidden, bins, sums, single):
    width = sums.shape[1]
    return pl.pallas_call(
        functools.partial(finish, 1.0 / tokens),
        out_shape=[
            jax.ShapeDtypeStruct((width, 2 * hidden), F32),
            jax.ShapeDtypeStruct((hidden, width), F32),
            jax.ShapeDtypeStruct((bins, width), F32),
            jax.ShapeDtypeStruct(single.shape, F32),
        ],
        in_specs=[VM] * 2,
        out_specs=[VM] * 4,
        name="finish",
    )(sums, single)


def local(
    n_row, n_col,
    singles, pair_in, proj_weight, gain_first, first_in, first_out, gain_second, second_in,
    second_out, head_weight, pae_bins, chain_perm, resolved_counts, tile_order,
):
    rows_dev, cols_dev, width = pair_in.shape
    hidden = first_out.shape[0]
    bins = head_weight.shape[1]
    left, right, target, live = run_prologue(
        n_row, n_col, singles.T, proj_weight, pae_bins.T, chain_perm.reshape(n_row, -1),
        resolved_counts, tile_order,
    )
    need = 3 * hidden + bins
    pay = -(-need // (16 * n_row)) * 16 * n_row
    pair_grad, left_part, right_part, weights = run_grid(
        pay, pair_in.reshape(rows_dev * cols_dev, width), left, right, target, live,
        gain_first.reshape(1, width), first_in, first_out,
        gain_second.reshape(1, width), second_in, second_out, head_weight.T,
    )
    sums, single = run_epilogue(n_row, n_col, weights, left_part, right_part, proj_weight)
    in_grad, out_grad, head_grad, single_grad = run_finish(
        chain_perm.shape[0], hidden, bins, sums, single
    )
    return (
        pair_grad.reshape(rows_dev, cols_dev, width), single_grad.T, in_grad, out_grad, head_grad.T,
    )


def solution(mesh):
    in_specs = (
        P("row", "col"), P("row", "col", None), P("col", None), P(), P(), P(), P(), P(), P(), P(),
        P("row", "col"), P(), P("row", None), P("row", "col"),
    )
    out_specs = (P("row", "col", None), P("row", "col"), P(), P(), P())
    body = functools.partial(local, mesh.shape["row"], mesh.shape["col"])
    return jax.shard_map(body, mesh=mesh, in_specs=in_specs, out_specs=out_specs, check_vma=False)
```

```python
import functools
import jax
import jax.numpy as jnp
from jax import lax
from jax.experimental import pallas as pl
from jax.experimental.pallas import tpu as pltpu
from jax.sharding import PartitionSpec as P

TILE = 32
BLOCK_PAIRS = 512
STREAMS = 4
CHUNK = 256
MESH = pl.DeviceIdType.MESH
BF = jnp.bfloat16
F32 = jnp.float32
VM = pl.BlockSpec(memory_space=pltpu.VMEM)
SM = pl.BlockSpec(memory_space=pltpu.SMEM)


def dot(left, right):
    return jnp.dot(left, right, preferred_element_type=F32)


def dot_rows(left, right):
    return lax.dot_general(left, right, (((0,), (0,)), ((), ())), preferred_element_type=F32)


def dot_lanes(left, right):
    return lax.dot_general(left, right, (((1,), (1,)), ((), ())), preferred_element_type=F32)


def prologue(
    n_row,
    n_col,
    singles,
    proj,
    bins,
    perm,
    counts,
    order,
    left_out,
    right_out,
    target_out,
    live_out,
    s_buf,
    w_buf,
    r_buf,
    r_full,
    s_send,
    s_recv,
    w_send,
    w_recv,
    r_send,
    r_recv,
):
    row, col = lax.axis_index("row"), lax.axis_index("col")
    chans = singles.shape[0]
    room = s_buf.shape[0] // n_col
    source_row = col // 2
    own_right = source_row == row
    s_buf[...] = jnp.zeros_like(s_buf)
    w_buf[...] = jnp.zeros_like(w_buf)
    r_buf[...] = jnp.zeros_like(r_buf)
    barrier = pltpu.get_barrier_semaphore()
    for k in range(1, n_col):
        peer = lax.rem(col + k, n_col)
        pl.semaphore_signal(barrier, inc=1, device_id=(row, peer), device_id_type=MESH)
        pl.semaphore_signal(barrier, inc=1, device_id=(source_row, peer), device_id_type=MESH)

    @pl.when(jnp.logical_not(own_right))
    def _():
        pl.semaphore_signal(barrier, inc=1, device_id=(source_row, col), device_id_type=MESH)

    pl.semaphore_wait(barrier, n_col - 1 + 2 * n_row - jnp.where(own_right, 1, 0))

    def spot(k):
        return pl.ds(k * room, chans)

    def s_copy(k):
        return pltpu.make_async_remote_copy(
            singles, s_buf.at[spot(k)], s_send.at[k], s_recv.at[k],
            device_id=(row, lax.rem(col + k, n_col)), device_id_type=MESH,
        )

    def w_copy(k):
        return pltpu.make_async_remote_copy(
            proj, w_buf.at[spot(k)], w_send.at[k], w_recv.at[k],
            device_id=(row, lax.rem(col + k, n_col)), device_id_type=MESH,
        )

    def r_copy(h, k):
        target = 2 * row + h
        slot = lax.rem(target - col + n_col, n_col)
        place = pl.ds(pl.multiple_of(slot * room, room), chans)
        return pltpu.make_async_remote_copy(
            singles, r_buf.at[place], r_send.at[h, k], r_recv.at[slot],
            device_id=(lax.rem(row + k, n_row), target), device_id_type=MESH,
        )

    def other(h):
        return col != 2 * row + h

    for k in range(1, n_col):
        w_copy(k).start()
        s_copy(k).start()
    for h in (0, 1):
        for k in range(1, n_row):
            r_copy(h, k).start()

        @pl.when(other(h))
        def _():
            r_copy(h, 0).start()

    s_buf[spot(0), :] = singles[...]
    w_buf[spot(0), :] = proj[...]

    @pl.when(own_right)
    def _():
        r_buf[spot(0), :] = singles[...]

    group = bins.shape[0]
    count = counts[0, col]
    tiles = order.shape[1]
    hit = order[...] == lax.broadcasted_iota(jnp.int32, (tiles, tiles), 0)
    chosen = lax.broadcasted_iota(jnp.int32, (tiles, live_out.shape[1]), 0) < count
    live_out[...] = dot(
        jnp.where(hit, 1.0, 0.0).astype(BF), jnp.where(chosen, 1.0, 0.0).astype(BF)
    )
    place = lax.broadcasted_iota(jnp.int32, (group, group), 0)
    pair_of = perm[pl.ds(source_row, 1), :]
    mine = jnp.where(lax.rem(col, 2) == 0, pair_of[:, :group], pair_of[:, group:])
    col_hit = jnp.where(mine - col * group == place, 1.0, 0.0).astype(BF)
    pair_of = perm[pl.ds(row, 1), :]
    step_rows = BLOCK_PAIRS // group
    for h in (0, 1):
        mine = pair_of[:, h * group : (h + 1) * group] - (2 * row + h) * group
        row_hit = jnp.where(mine == place, 1.0, 0.0).astype(BF)
        part = bins[:, h * group : (h + 1) * group].astype(F32).astype(BF)
        wanted = dot_rows(row_hit, dot_rows(part, col_hit).astype(BF))
        for b in range(group // step_rows):
            lanes = [wanted[b * step_rows + i : b * step_rows + i + 1, :] for i in range(step_rows)]
            target_out[h * (group // step_rows) + b] = jnp.concatenate(lanes, axis=1)

    width = proj.shape[1] // 2
    for k in range(1, n_col):
        w_copy(k).wait()
        s_copy(k).wait()
    left_out[...] = dot_rows(s_buf[...], w_buf[:, :width])

    def arrived(k):
        return pltpu.make_async_remote_copy(
            singles, r_buf.at[spot(k)], r_send.at[0, 0], r_recv.at[k],
            device_id=(row, col), device_id_type=MESH,
        )

    @pl.when(jnp.logical_not(own_right))
    def _():
        arrived(0).wait_recv()

    for k in range(1, n_col):
        arrived(k).wait_recv()
    r_full[...] = dot_rows(r_buf[...], w_buf[:, width:]).astype(BF).astype(F32)
    half = right_out.shape[0]
    right_out[...] = r_full[pl.ds(pl.multiple_of(lax.rem(col, 2) * half, half), half), :]
    for h in (0, 1):
        for k in range(1, n_row):
            r_copy(h, k).wait_send()

        @pl.when(other(h))
        def _():
            r_copy(h, 0).wait_send()


def run_prologue(n_row, n_col, singles, proj, bins, perm, counts, order):
    chans, rows_dev = singles.shape
    wide = proj.shape[1]
    width = wide // 2
    cols_dev = bins.shape[0]
    tiles = order.shape[1]
    blocks = rows_dev * cols_dev // BLOCK_PAIRS
    room = -(-chans // 16) * 16
    dma = pltpu.SemaphoreType.DMA
    return pl.pallas_call(
        functools.partial(prologue, n_row, n_col),
        out_shape=[
            jax.ShapeDtypeStruct((rows_dev, width), F32),
            jax.ShapeDtypeStruct((cols_dev, width), F32),
            jax.ShapeDtypeStruct((blocks, 1, BLOCK_PAIRS), F32),
            jax.ShapeDtypeStruct((tiles, width), F32),
        ],
        in_specs=[VM, VM, VM, VM, SM, VM],
        out_specs=[VM] * 4,
        scratch_shapes=[
            pltpu.VMEM((n_col * room, rows_dev), BF),
            pltpu.VMEM((n_col * room, wide), BF),
            pltpu.VMEM((n_col * room, rows_dev), BF),
            pltpu.VMEM((rows_dev, width), F32),
            dma((n_col,)), dma((n_col,)), dma((n_col,)), dma((n_col,)),
            dma((2, n_row)), dma((n_col,)),
        ],
        compiler_params=pltpu.CompilerParams(collective_id=0, has_side_effects=True),
        name="prologue",
    )(singles, proj, bins, perm, counts, order)


def layer_norm(field):
    centred = field - jnp.mean(field, axis=-1, keepdims=True)
    scaling = lax.rsqrt(jnp.mean(centred * centred, axis=-1, keepdims=True) + 1e-05)
    return centred * scaling, scaling


def forward(inputs, w_in, w_out, a_ref, d_ref, h_ref):
    hidden = w_out.shape[0]
    total = None
    for c in range(0, hidden, CHUNK):
        here = pl.ds(c, CHUNK)
        gate = dot(inputs, w_in[:, here]).astype(BF)
        up = dot(inputs, w_in[:, pl.ds(hidden + c, CHUNK)]).astype(BF)
        low = gate * BF(0.5)
        twice = jnp.tanh(low) + BF(1)
        act = low * twice
        slope = act + (BF(0.5) * twice) * (BF(1) - act)
        value = act * up
        a_ref[:, here] = act
        d_ref[:, here] = up * slope
        if h_ref is not None:
            h_ref[:, here] = value
        part = dot(value, w_out[here, :])
        total = part if total is None else total + part
    return total


def backward(cot, w_in, w_out, a_ref, d_ref, b_ref):
    hidden = w_out.shape[0]
    total = None
    for c in range(0, hidden, CHUNK):
        here = pl.ds(c, CHUNK)
        there = pl.ds(hidden + c, CHUNK)
        grad_hidden = dot_lanes(cot, w_out[here, :]).astype(BF)
        grad_gate = grad_hidden * d_ref[:, here]
        grad_up = grad_hidden * a_ref[:, here]
        if b_ref is not None:
            b_ref[:, here] = grad_gate
            b_ref[:, there] = grad_up
        part = dot_lanes(grad_gate, w_in[:, here]) + dot_lanes(grad_up, w_in[:, there])
        total = part if total is None else total + part
    return total


def norm_backward(grad, gain, normed, scaling):
    grad = grad * gain
    return scaling * (
        grad
        - jnp.mean(grad, axis=-1, keepdims=True)
        - normed * jnp.mean(grad * normed, axis=-1, keepdims=True)
    )


def stream(
    here, pair, left, right, target, live, g1, w1, w1o, g2, w2, w2o, head,
    pair_grad, left_grad, right_grad, in_acc, out_acc, head_acc,
    a1, d1, a2, d2, h2, b2, n1,
):
    rows_here, tiles_here = here[1], here[2]
    width = pair.shape[1]
    cols = right.shape[0]
    pairs = here[0].size
    rows = pairs // cols
    field = pair[here[0], :].astype(F32).reshape(rows, cols, width)
    field = (field + left[rows_here, :][:, None, :] + right[...][None]).reshape(pairs, width)
    normed, s1 = layer_norm(field)
    n1[...] = normed
    inputs1 = (normed * g1[...]).astype(BF)
    yield
    delta = forward(inputs1, w1, w1o, a1, d1, None)
    yield
    second = (field + delta).astype(BF).astype(F32)
    normed2, s2 = layer_norm(second)
    inputs2 = (normed2 * g2[...]).astype(BF)
    yield
    delta2 = forward(inputs2, w2, w2o, a2, d2, h2)
    yield
    tiles = tiles_here.size
    mask = jnp.broadcast_to(live[tiles_here, :][:, None, :], (tiles, pairs // tiles, width))
    mask = mask.reshape(pairs, width)
    last = (second + mask * delta2).astype(BF)
    logits = dot_lanes(head[...], last)
    exponent = jnp.exp(logits - jnp.max(logits, axis=0, keepdims=True))
    prob = exponent / jnp.sum(exponent, axis=0, keepdims=True)
    bin_id = lax.broadcasted_iota(jnp.int32, logits.shape, 0).astype(F32)
    grad_logits = (prob - jnp.where(target[here[3]] == bin_id, 1.0, 0.0)).astype(BF)
    head_acc[...] += dot(grad_logits, last)
    grad_two = dot_rows(grad_logits, head[...]).astype(BF).astype(F32)
    cot2 = jnp.where(mask > 0, grad_two, 0.0).astype(BF)
    yield
    normed_grad = backward(cot2, w2, w2o, a2, d2, b2)
    yield
    in_acc[...] += dot_rows(inputs2, b2[...])
    out_acc[...] += dot_rows(cot2, h2[...])
    grad_one = (grad_two + norm_backward(normed_grad, g2[...], normed2, s2)).astype(BF)
    yield
    normed_grad = backward(grad_one, w1, w1o, a1, d1, None)
    yield
    grad_zero = grad_one.astype(F32) + norm_backward(normed_grad, g1[...], n1[...], s1)
    pair_grad[here[0], :] = grad_zero.astype(BF)
    grid = grad_zero.reshape(rows, cols, width)
    right_grad[...] += jnp.sum(grid, axis=0)
    left_grad[rows_here, :] = jnp.sum(grid, axis=1)
    yield


def grid_step(
    pair, left, right, target, live, g1, w1, w1o, g2, w2, w2o, head,
    pair_grad, left_grad, right_grad, weight_out, in_acc, out_acc, head_acc, *scratch,
):
    width = pair.shape[1]
    step = pl.program_id(0)

    @pl.when(step == 0)
    def _():
        right_grad[...] = jnp.zeros_like(right_grad)
        in_acc[...] = jnp.zeros_like(in_acc)
        out_acc[...] = jnp.zeros_like(out_acc)
        head_acc[...] = jnp.zeros_like(head_acc)

    each = len(scratch) // STREAMS
    pairs, rows = BLOCK_PAIRS, left.shape[0] // STREAMS
    tiles = live.shape[0] // STREAMS
    streams = []
    for k in range(STREAMS):
        here = (pl.ds(k * pairs, pairs), pl.ds(k * rows, rows), pl.ds(k * tiles, tiles), k)
        streams.append(
            stream(
                here, pair, left, right, target, live, g1, w1, w1o, g2, w2, w2o, head,
                pair_grad, left_grad, right_grad, in_acc, out_acc, head_acc,
                *scratch[k * each : (k + 1) * each],
            )
        )
    for _ in zip(*streams):
        pass

    @pl.when(step == pl.num_programs(0) - 1)
    def _():
        wide = in_acc.shape[1] // width
        for j in range(wide):
            weight_out[j * width : (j + 1) * width, :] = in_acc[:, j * width : (j + 1) * width].astype(BF)
        base = wide * width
        more = out_acc.shape[1] // width
        for j in range(more):
            block = out_acc[:, j * width : (j + 1) * width].T.astype(BF)
            weight_out[base + j * width : base + (j + 1) * width, :] = block
        base = base + more * width
        bins = head_acc.shape[0]
        weight_out[base : base + bins, :] = head_acc[...].astype(BF)
        rest = weight_out.shape[0] - base - bins
        weight_out[base + bins :, :] = jnp.zeros((rest, width), BF)


def run_grid(pay_rows, pair, left, right, target, live, g1, w1, w1o, g2, w2, w2o, head):
    pairs, width = pair.shape
    cols = right.shape[0]
    size = BLOCK_PAIRS * STREAMS
    steps = pairs // size
    rows = size // cols
    tiles = live.shape[0] // steps
    hidden = w1o.shape[0]
    bins = head.shape[0]

    def full(shape):
        return pl.BlockSpec(shape, lambda i: (0,) * len(shape))

    def part(shape):
        return pl.BlockSpec(shape, lambda i: (i,) + (0,) * (len(shape) - 1))

    return pl.pallas_call(
        grid_step,
        grid=(steps,),
        in_specs=[
            part((size, width)), part((rows, width)), full((cols, width)), part((STREAMS, 1, BLOCK_PAIRS)),
            part((tiles, width)), full((1, width)), full(w1.shape), full(w1o.shape),
            full((1, width)), full(w2.shape), full(w2o.shape), full(head.shape),
        ],
        out_specs=[
            part((size, width)), part((rows, width)), full((cols, width)), full((pay_rows, width)),
        ],
        out_shape=[
            jax.ShapeDtypeStruct((pairs, width), BF),
            jax.ShapeDtypeStruct((pairs // cols, width), F32),
            jax.ShapeDtypeStruct((cols, width), F32),
            jax.ShapeDtypeStruct((pay_rows, width), BF),
        ],
        scratch_shapes=[
            pltpu.VMEM((width, 2 * hidden), F32),
            pltpu.VMEM((width, hidden), F32),
            pltpu.VMEM((bins, width), F32),
        ]
        + (
            [pltpu.VMEM((BLOCK_PAIRS, hidden), BF)] * 5
            + [pltpu.VMEM((BLOCK_PAIRS, 2 * hidden), BF), pltpu.VMEM((BLOCK_PAIRS, width), F32)]
        )
        * STREAMS,
        compiler_params=pltpu.CompilerParams(dimension_semantics=("arbitrary",)),
        name="grid",
    )(pair, left, right, target, live, g1, w1, w1o, g2, w2, w2o, head)


def epilogue(
    n_row, n_col,
    weights, left_part, right_part, proj,
    final, single_out,
    in1, tok1, mid, tok_mid, in2, left2, right_all, left_all, gathered,
    send1, recv1, tsend1, trecv1, send2, recv2, lsend2, lrecv2, rsend, rrecv,
    send3, recv3, lsend3, lrecv3, send4, recv4, fsem,
):
    row, col = lax.axis_index("row"), lax.axis_index("col")
    width = weights.shape[1]
    share = weights.shape[0] // n_row
    small = mid.shape[0] // n_col
    tok = tok1.shape[1]
    target_row = col // 2
    self_case = target_row == row
    barrier = pltpu.get_barrier_semaphore()
    for k in range(1, n_row):
        peer = lax.rem(row + k, n_row)
        pl.semaphore_signal(barrier, inc=1, device_id=(peer, col), device_id_type=MESH)
        for h in (0, 1):
            pl.semaphore_signal(barrier, inc=1, device_id=(peer, 2 * row + h), device_id_type=MESH)
    for k in range(1, n_col):
        peer = lax.rem(col + k, n_col)
        pl.semaphore_signal(barrier, inc=1, device_id=(row, peer), device_id_type=MESH)
    for h in (0, 1):

        @pl.when(col != 2 * row + h)
        def _():
            pl.semaphore_signal(barrier, inc=1, device_id=(row, 2 * row + h), device_id_type=MESH)

    pl.semaphore_wait(barrier, n_row + n_col + n_col - 2 - jnp.where(self_case, 1, 0))

    def row_peer(k):
        return lax.rem(row + k, n_row)

    def col_peer(k):
        return lax.rem(col + k, n_col)

    def copy1(k):
        start = pl.multiple_of(row_peer(k) * share, share)
        return pltpu.make_async_remote_copy(
            weights.at[pl.ds(start, share)], in1.at[k], send1.at[k], recv1.at[k],
            device_id=(row_peer(k), col), device_id_type=MESH,
        )

    def tcopy1(k):
        start = pl.multiple_of(row_peer(k) * tok, tok)
        return pltpu.make_async_remote_copy(
            right_part.at[pl.ds(start, tok)], tok1.at[k], tsend1.at[k], trecv1.at[k],
            device_id=(row_peer(k), col), device_id_type=MESH,
        )

    def lcopy2(k):
        start = pl.multiple_of(col_peer(k) * tok, tok)
        return pltpu.make_async_remote_copy(
            left_part.at[pl.ds(start, tok)], left2.at[k], lsend2.at[k], lrecv2.at[k],
            device_id=(row, col_peer(k)), device_id_type=MESH,
        )

    for k in range(1, n_row):
        copy1(k).start()
        tcopy1(k).start()
    for k in range(1, n_col):
        lcopy2(k).start()

    own = right_part[pl.ds(pl.multiple_of(row * tok, tok), tok), :]
    for k in range(1, n_row):
        tcopy1(k).wait()
        own += tok1[k]
    tok_mid[...] = own
    slot = lax.rem(col, 2) * n_row + row

    def rcopy(k):
        return pltpu.make_async_remote_copy(
            tok_mid, right_all.at[slot], rsend.at[k], rrecv.at[slot],
            device_id=(target_row, col_peer(k)), device_id_type=MESH,
        )

    for k in range(1, n_col):
        rcopy(k).start()

    @pl.when(jnp.logical_not(self_case))
    def _():
        rcopy(0).start()

    own = left_part[pl.ds(pl.multiple_of(col * tok, tok), tok), :]
    for k in range(1, n_col):
        lcopy2(k).wait()
        own += left2[k]
    left_all[col] = own

    def lcopy3(k):
        return pltpu.make_async_remote_copy(
            left_all.at[col], left_all.at[col], lsend3.at[k], lrecv3.at[col],
            device_id=(row, col_peer(k)), device_id_type=MESH,
        )

    for k in range(1, n_col):
        lcopy3(k).start()

    total = weights[pl.ds(pl.multiple_of(row * share, share), share), :].astype(F32)
    for k in range(1, n_row):
        copy1(k).wait()
        total += in1[k].astype(F32)
    mid[:share, :] = total.astype(BF)
    mid[share:, :] = jnp.zeros((mid.shape[0] - share, width), BF)

    def copy2(k):
        start = pl.multiple_of(col_peer(k) * small, small)
        return pltpu.make_async_remote_copy(
            mid.at[pl.ds(start, small)], in2.at[k], send2.at[k], recv2.at[k],
            device_id=(row, col_peer(k)), device_id_type=MESH,
        )

    for k in range(1, n_col):
        copy2(k).start()
    total = mid[pl.ds(pl.multiple_of(col * small, small), small), :].astype(F32)
    for k in range(1, n_col):
        copy2(k).wait()
        total += in2[k].astype(F32)
    mine = pl.ds(pl.multiple_of(col * small, small), small)
    gathered[mine, :] = total.astype(BF)

    def copy3(k):
        return pltpu.make_async_remote_copy(
            gathered.at[mine], gathered.at[mine], send3.at[k], recv3.at[col],
            device_id=(row, col_peer(k)), device_id_type=MESH,
        )

    def came3(j):
        spot = pl.ds(pl.multiple_of(j * small, small), small)
        return pltpu.make_async_remote_copy(
            gathered.at[spot], gathered.at[spot], send3.at[0], recv3.at[j],
            device_id=(row, j), device_id_type=MESH,
        )

    for k in range(1, n_col):
        copy3(k).start()
    for k in range(1, n_col):
        came3(col_peer(k)).wait_recv()
    for k in range(1, n_col):
        copy3(k).wait_send()

    band = pl.ds(pl.multiple_of(row * share, share), share)

    def copy4(k):
        return pltpu.make_async_remote_copy(
            gathered.at[pl.ds(0, share)], final.at[band], send4.at[k], recv4.at[row],
            device_id=(row_peer(k), col), device_id_type=MESH,
        )

    def came4(j):
        spot = pl.ds(pl.multiple_of(j * share, share), share)
        return pltpu.make_async_remote_copy(
            gathered.at[pl.ds(0, share)], final.at[spot], send4.at[0], recv4.at[j],
            device_id=(j, col), device_id_type=MESH,
        )

    for k in range(1, n_row):
        copy4(k).start()
    own_copy = pltpu.make_async_copy(gathered.at[pl.ds(0, share)], final.at[band], fsem)
    own_copy.start()

    def lcame(j):
        return pltpu.make_async_remote_copy(
            left_all.at[j], left_all.at[j], lsend3.at[0], lrecv3.at[j],
            device_id=(row, j), device_id_type=MESH,
        )

    def rcame(j):
        return pltpu.make_async_remote_copy(
            tok_mid, right_all.at[j], rsend.at[0], rrecv.at[j],
            device_id=(row, col), device_id_type=MESH,
        )

    for k in range(1, n_col):
        lcame(col_peer(k)).wait_recv()
        lcopy3(k).wait_send()
        rcopy(k).wait_send()

    @pl.when(jnp.logical_not(self_case))
    def _():
        rcopy(0).wait_send()

    for k in range(1, n_col):
        rcame(lax.rem(slot + k, n_col)).wait_recv()

    @pl.when(jnp.logical_not(self_case))
    def _():
        rcame(slot).wait_recv()

    @pl.when(self_case)
    def _():
        right_all[slot] = tok_mid[...]

    tokens = n_col * tok
    left_tok = left_all[...].reshape(tokens, width).astype(BF)
    right_tok = right_all[...].reshape(tokens, width).astype(BF)
    single_out[...] = dot_lanes(proj[:, :width], left_tok) + dot_lanes(proj[:, width:], right_tok)

    own_copy.wait()
    for k in range(1, n_row):
        came4(row_peer(k)).wait_recv()
    for k in range(1, n_row):
        copy4(k).wait_send()


def run_epilogue(n_row, n_col, weights, left_part, right_part, proj):
    width = weights.shape[1]
    pay = weights.shape[0]
    share = pay // n_row
    rows_dev = left_part.shape[0]
    tok = rows_dev // n_col
    small = -(-share // (16 * n_col)) * 16
    dma = pltpu.SemaphoreType.DMA
    sems = [
        n_row, n_row, n_row, n_row, n_col, n_col, n_col, n_col, n_col, n_col,
        n_col, n_col, n_col, n_col, n_row, n_row,
    ]
    return pl.pallas_call(
        functools.partial(epilogue, n_row, n_col),
        out_shape=[
            jax.ShapeDtypeStruct((pay, width), BF),
            jax.ShapeDtypeStruct((proj.shape[0], rows_dev), F32),
        ],
        in_specs=[VM] * 4,
        out_specs=[VM] * 2,
        scratch_shapes=[
            pltpu.VMEM((n_row, share, width), BF),
            pltpu.VMEM((n_row, tok, width), F32),
            pltpu.VMEM((small * n_col, width), BF),
            pltpu.VMEM((tok, width), F32),
            pltpu.VMEM((n_col, small, width), BF),
            pltpu.VMEM((n_col, tok, width), F32),
            pltpu.VMEM((n_col, tok, width), F32),
            pltpu.VMEM((n_col, tok, width), F32),
            pltpu.VMEM((small * n_col, width), BF),
        ]
        + [dma((n,)) for n in sems]
        + [dma],
        compiler_params=pltpu.CompilerParams(collective_id=1, has_side_effects=True),
        name="epilogue",
    )(weights, left_part, right_part, proj)


def finish(scale, sums, single, in_out, out_out, head_out, single_out):
    width = sums.shape[1]
    wide = in_out.shape[1] // width
    for j in range(wide):
        block = sums[j * width : (j + 1) * width, :].astype(F32) * scale
        in_out[:, j * width : (j + 1) * width] = block
    base = wide * width
    hidden = out_out.shape[0]
    out_out[...] = sums[base : base + hidden, :].astype(F32) * scale
    bins = head_out.shape[0]
    head_out[...] = sums[base + hidden : base + hidden + bins, :].astype(F32) * scale
    single_out[...] = single[...]


def run_finish(tokens, hidden, bins, sums, single):
    width = sums.shape[1]
    return pl.pallas_call(
        functools.partial(finish, 1.0 / tokens),
        out_shape=[
            jax.ShapeDtypeStruct((width, 2 * hidden), F32),
            jax.ShapeDtypeStruct((hidden, width), F32),
            jax.ShapeDtypeStruct((bins, width), F32),
            jax.ShapeDtypeStruct(single.shape, F32),
        ],
        in_specs=[VM] * 2,
        out_specs=[VM] * 4,
        name="finish",
    )(sums, single)


def local(
    n_row, n_col,
    singles, pair_in, proj_weight, gain_first, first_in, first_out, gain_second, second_in,
    second_out, head_weight, pae_bins, chain_perm, resolved_counts, tile_order,
):
    rows_dev, cols_dev, width = pair_in.shape
    hidden = first_out.shape[0]
    bins = head_weight.shape[1]
    left, right, target, live = run_prologue(
        n_row, n_col, singles.T, proj_weight, pae_bins.T, chain_perm.reshape(n_row, -1),
        resolved_counts, tile_order,
    )
    need = 3 * hidden + bins
    pay = -(-need // (16 * n_row)) * 16 * n_row
    pair_grad, left_part, right_part, weights = run_grid(
        pay, pair_in.reshape(rows_dev * cols_dev, width), left, right, target, live,
        gain_first.reshape(1, width), first_in, first_out,
        gain_second.reshape(1, width), second_in, second_out, head_weight.T,
    )
    sums, single = run_epilogue(n_row, n_col, weights, left_part, right_part, proj_weight)
    in_grad, out_grad, head_grad, single_grad = run_finish(
        chain_perm.shape[0], hidden, bins, sums, single
    )
    return (
        pair_grad.reshape(rows_dev, cols_dev, width), single_grad.T, in_grad, out_grad, head_grad.T,
    )


def solution(mesh):
    in_specs = (
        P("row", "col"), P("row", "col", None), P("col", None), P(), P(), P(), P(), P(), P(), P(),
        P("row", "col"), P(), P("row", None), P("row", "col"),
    )
    out_specs = (P("row", "col", None), P("row", "col"), P(), P(), P())
    body = functools.partial(local, mesh.shape["row"], mesh.shape["col"])
    return jax.shard_map(body, mesh=mesh, in_specs=in_specs, out_specs=out_specs, check_vma=False)
```
